512 devices in a mesh: atom: 64 (over y_lo, z, core), kvec: 8 (over y_hi, x).
Axes of the slice: x: 4, y: 4 (y_hi: 2, y_lo: 2; y = y_hi * 2 + y_lo), z: 16, core: 2. Of those that a mesh axis runs over, the one named last changes fastest.
Arguments:
- features: bfloat16 [64, 24576], P(None, 'atom'), may hold values from -6 to 6
- species: int32 [24576], P('atom'), may hold values from 0 to 3
- embed: float32 [4, 64], replicated, may hold values from -4 to 4
- frac_pos: float32 [3, 24576], P(None, 'atom'), may hold values from 0 to 1
- box: float32 [3], replicated, may hold values from 105 to 115
- miller: int32 [3, 8192], P(None, 'kvec'), may hold values from -40 to 40
- filter_weight: float32 [16, 64], replicated, may hold values from -1.5 to 1.5
- cotangent: bfloat16 [64, 24576], P(None, 'atom'), may hold values from -6 to 6
Outputs:
- feat_grad: float32 [64, 24576], P(None, ('atom', 'kvec'))
- force: float32 [3, 24576], P(None, ('atom', 'kvec'))
- filter_grad: float32 [16, 64], replicated
- virial: float32 [3, 3], replicated
The draws below stay inside these ranges and needn't reach their ends.
All inputs are finite; a program needn't handle non-finite values.
Results may differ from the reference program's by a relative error of at most 0.0051.
Values may be sent and summed in bfloat16 or wider, within the bound.
A program may use at most 64 MiB of HBM per device.

```python
import math
import jax
import jax.numpy as jnp
import numpy as np
from jax import lax

C = 64
K = 8192
NB = 16
NSPEC = 4
MMAX = 40
NATOMS = 24576


def touch_ends(result, own_key, smallest, largest):
    longest = result.shape.index(max(result.shape))
    spots = []
    for shift in (0, 1):
        where = [jax.random.randint(jax.random.fold_in(own_key, axis), (), 0, length) for axis, length in enumerate(result.shape)]
        where[longest] = (where[longest] + shift) % result.shape[longest]
        spots.append(tuple(where))
    return result.at[spots[0]].set(smallest).at[spots[1]].set(largest)


def shard_levels(stream_key, shape, pieces, least, high):
    def one(axis_at, shards_of):
        draws = jax.random.uniform(jax.random.fold_in(jax.random.fold_in(stream_key, 6), axis_at), (shards_of,), jnp.float32, least / len(pieces), high / len(pieces))
        return jnp.repeat(jnp.exp(draws), shape[axis_at] // shards_of).reshape((-1,) + (1,) * (len(shape) - axis_at - 1))

    factor_of = one(*pieces[0])
    for cut in pieces[1:]:
        factor_of = factor_of * one(*cut)
    return factor_of


def cumulative_ranks(number_of, lean):
    loads = [(1 << 20) // math.isqrt(rank ** lean) + 1 for rank in range(1, number_of + 1)]
    scale = 1 + sum(loads) // (1 << 30)
    return np.cumsum(np.array([max(1, weight // scale) for weight in loads]))


def skewed_ids(stream_key, extent, amount, lean):
    grid = cumulative_ranks(amount, lean)
    pick = jax.random.randint(jax.random.fold_in(stream_key, 1), extent, 0, int(grid[amount - 1]))
    standing = jnp.searchsorted(jnp.asarray(grid, jnp.int32), pick, side="right")
    return jax.random.permutation(jax.random.fold_in(stream_key, 2), amount)[standing].astype(jnp.int32)


def centred(rng, extent, spread, reach, pieces=(), kind=jnp.bfloat16):
    loudness = shard_levels(rng, extent, pieces, -0.22, 0.18) if pieces else 1.0
    entries = jax.random.normal(rng, extent, jnp.float32) * spread * loudness
    return jnp.minimum(jnp.maximum(entries, -reach), reach).astype(kind)


def setup_inputs(seed: int = 0) -> dict:
    splits = jax.random.split(jax.random.key(seed), 9)
    return {
        "features": centred(splits[0], (C, NATOMS), 1.0, 6.0, ((1, 64),)),
        "species": touch_ends(skewed_ids(splits[1], (NATOMS,), NSPEC, 2), jax.random.fold_in(splits[1], 3), 0, NSPEC - 1).astype(jnp.int32),
        "embed": centred(splits[2], (NSPEC, C), 1.0, 4.0, (), jnp.float32),
        "frac_pos": jnp.clip(1.0 * jax.random.uniform(splits[3], (3, NATOMS), jnp.float32) ** shard_levels(splits[3], (3, NATOMS), ((1, 64),), -0.2, 0.2), 0.0, 1.0),
        "box": jnp.clip(jax.random.uniform(splits[4], (3,), jnp.float32, 105.0, 115.0), 105.0, 115.0),
        "miller": touch_ends(jax.random.randint(splits[5], (3, K), 0 - MMAX, MMAX + 1), jax.random.fold_in(splits[5], 1), 0 - MMAX, MMAX).astype(jnp.int32),
        "filter_weight": centred(splits[6], (NB, C), NB ** -0.5, 1.5, (), jnp.float32),
        "cotangent": centred(splits[7], (C, NATOMS), 1.0, 6.0, ((1, 64),)),
    }


TWO_PI = 2.0 * math.pi
PRECISE = lax.Precision.HIGHEST

def radial(q_vals, nbasis):
    q_top = 3.0 * (TWO_PI * MMAX / 105.0) ** 2
    centers = q_top * jnp.arange(nbasis, dtype=jnp.float32) / (nbasis - 1)
    spread_q = 1.5 * q_top / (nbasis - 1)
    offsets = (q_vals[None, :] - centers[:, None]) / spread_q
    radial_basis = jnp.exp(-offsets * offsets)
    radial_slope = -2.0 * offsets / spread_q * radial_basis
    return (radial_basis, radial_slope)

def phases(frac_pos, mill_block):
    m_vals = mill_block.astype(jnp.float32)
    phase_angle = TWO_PI * (frac_pos[0][:, None] * m_vals[0][None, :] + frac_pos[1][:, None] * m_vals[1][None, :] + frac_pos[2][:, None] * m_vals[2][None, :])
    return (jnp.cos(phase_angle).astype(jnp.bfloat16), jnp.sin(phase_angle).astype(jnp.bfloat16))

def kterms(factors, kvec, filter_weight, grad_scale):
    q_vals = kvec[0] * kvec[0] + kvec[1] * kvec[1] + kvec[2] * kvec[2]
    radial_basis, radial_slope = radial(q_vals, filter_weight.shape[0])
    filter_k = jnp.dot(filter_weight.T, radial_basis, precision=PRECISE)
    filter_slope = jnp.dot(filter_weight.T, radial_slope, precision=PRECISE)
    filtered = (filter_k[None] * factors).astype(jnp.bfloat16)
    energy = factors[0] * factors[2] + factors[1] * factors[3]
    filter_grad = lax.dot_general(radial_basis, energy, (((1,), (1,)), ((), ())), precision=PRECISE) * grad_scale
    weight_k = lax.optimization_barrier(jnp.sum(filter_slope * energy, axis=0))
    virial = -2.0 * grad_scale * jnp.dot(kvec * weight_k[None, :], kvec.T, precision=PRECISE)
    return (filtered, filter_grad, virial)

def reference(features, species, embed, frac_pos, box, miller, filter_weight, cotangent):
    channels = features.shape[0]
    hidden = (features.astype(jnp.float32) + jnp.take(embed, species, axis=0).T).astype(jnp.bfloat16)
    stacked = jnp.concatenate([hidden, cotangent], axis=0)
    kvec = TWO_PI * miller.astype(jnp.float32) / box[:, None]
    block_len = min(512, K)
    block_count = K // block_len
    mill_blocks = miller.reshape(3, block_count, block_len).transpose(1, 0, 2)

    def pass_one(mill_block):
        cos_tile, sin_tile = phases(frac_pos, mill_block)
        cos_part = jnp.dot(stacked, cos_tile, preferred_element_type=jnp.float32)
        sin_part = jnp.dot(stacked, sin_tile, preferred_element_type=jnp.float32)
        return jnp.stack([cos_part[:channels], sin_part[:channels], cos_part[channels:], sin_part[channels:]])
    factors = lax.map(pass_one, mill_blocks)
    factors = factors.transpose(1, 2, 0, 3).reshape(4, channels, K) / math.sqrt(NATOMS)
    grad_scale = math.sqrt(NATOMS) / math.sqrt(K)
    filtered, filter_grad, virial = kterms(factors, kvec, filter_weight, grad_scale)
    filt_blocks = filtered.reshape(4, channels, block_count, block_len).transpose(2, 0, 1, 3)
    kvec_blocks = kvec.reshape(3, block_count, block_len).transpose(1, 0, 2)
    dims_k = (((1,), (1,)), ((), ()))
    dims_c = (((0,), (0,)), ((), ()))

    def pass_two(totals, inputs):
        feat_acc, force_acc = totals
        mill_block, filt_block, kvec_block = inputs
        cos_tile, sin_tile = phases(frac_pos, mill_block)
        feat_acc = feat_acc + lax.dot_general(filt_block[2], cos_tile, dims_k, preferred_element_type=jnp.float32) + lax.dot_general(filt_block[3], sin_tile, dims_k, preferred_element_type=jnp.float32)
        along_cos = lax.dot_general(stacked, jnp.concatenate([filt_block[3], filt_block[1]], axis=0), dims_c, preferred_element_type=jnp.float32)
        along_sin = lax.dot_general(stacked, jnp.concatenate([filt_block[2], filt_block[0]], axis=0), dims_c, preferred_element_type=jnp.float32)
        dphase = (cos_tile.astype(jnp.float32) * along_cos - sin_tile.astype(jnp.float32) * along_sin) / math.sqrt(K)
        force_acc = force_acc - lax.dot_general(kvec_block, dphase, dims_k, precision=PRECISE)
        return ((feat_acc, force_acc), None)
    start_acc = (jnp.zeros((channels, NATOMS), jnp.float32), jnp.zeros((3, NATOMS), jnp.float32))
    (feat_acc, force), unused = lax.scan(pass_two, start_acc, (mill_blocks, filt_blocks, kvec_blocks))
    feat_grad = feat_acc / math.sqrt(K)
    return (feat_grad, force, filter_grad, virial)
```

```python
import functools
import math

import jax
import jax.numpy as jnp
import numpy as np
from jax import lax
from jax.experimental import pallas as pl
from jax.experimental.pallas import tpu as pltpu
from jax.sharding import PartitionSpec as P

K = 8192
MMAX = 40
TWO_PI = 2.0 * math.pi
PRECISE = lax.Precision.HIGHEST
MESH = pl.DeviceIdType.MESH
F32, BF16 = jnp.float32, jnp.bfloat16
MAGIC = 12582912.0

NZ = 16
NX = 4
NV = 8
CH = 4
ATOMS = 384
KL = 256
PIECE = 48

NN = (((1,), (0,)), ((), ()))
NT = (((1,), (1,)), ((), ()))
TN = (((0,), (0,)), ((), ()))


def _fit(fn, degree):
    n = 64
    nodes = 0.125 + 0.125 * np.cos(np.pi * (np.arange(n) + 0.5) / n)
    cheb = np.polynomial.chebyshev.Chebyshev.fit(nodes, fn(np.sqrt(nodes)), degree, domain=[0.0, 0.25])
    return [float(c) for c in cheb.convert(kind=np.polynomial.Polynomial).coef]


ROOT2 = math.sqrt(2.0)
SIN_C = _fit(lambda r: ROOT2 * np.sin(np.pi * r) / r, 4)
COS_C = _fit(lambda r: ROOT2 * np.cos(np.pi * r), 4)


def horner(u, coef):
    acc = coef[-1] * u + coef[-2]
    for c in coef[-3::-1]:
        acc = acc * u + c
    return acc


def cos_sin_turns(t):
    r = t - ((t + MAGIC) - MAGIC)
    u = r * r
    s = r * horner(u, SIN_C)
    c = horner(u, COS_C)
    return 1.0 - s * s, s * c


def dot(a, b, dims=NN, precision=None):
    return lax.dot_general(a, b, dims, preferred_element_type=F32, precision=precision)


def iota(shape, axis):
    return lax.broadcasted_iota(jnp.int32, shape, axis)


def select(cond):
    return jnp.where(cond, 1.0, 0.0).astype(BF16)


def kernel(
    feat_ref, spec_ref, emb_ref, frac_ref, box_ref, mil_ref, w_ref, cot_ref,
    feat_out, force_out, wgrad_out, vir_out,
    gbuf, pos_s, cbuf, sbuf, tcbuf, tsbuf, tbuf, mrep, wm_s, bk_s, filt, slope, facc,
    rs_snd, rs_buf, ag_buf, pl_snd, pl_buf, zs_buf, fg_s, alc, als, dbuf, fin_snd, fin_buf,
    g_ss, g_rs, rs_ss, rs_rs, ag_ss, ag_rs, pl_ss, pl_rs, zs_ss, zs_rs, fin_ss, fin_rs,
):
    a = lax.axis_index("atom")
    v = lax.axis_index("kvec")
    y_lo = a // (2 * NZ)
    z = (a // 2) % NZ
    core = a % 2
    y_hi = v // NX
    x = v % NX
    mine = y_lo * 2 + core

    def device(yl, zz, cc, vv):
        return {"atom": (yl * NZ + zz) * 2 + cc, "kvec": vv}

    def z_peer(i):
        return device(y_lo, (z + i) % NZ, core, v)

    def plane_peer(p, q, j):
        return device((y_lo + p) % 2, z, (core + q) % 2, (v + j) % NV)

    far_first = [8, 7, 9, 6, 10, 5, 11, 4, 12, 3, 13, 2, 14, 1, 15]
    plane = [(p, q, j) for p in (1, 0) for q in (1, 0) for j in (4, 6, 2, 5, 7, 3, 1, 0)]
    plane = [t for t in plane if t != (0, 0, 0)]

    def plane_slot(p, q, j):
        return (p * 2 + q) * 8 + j

    def send(src, dst, ss, rs, dev):
        cp = pltpu.make_async_remote_copy(
            src_ref=src, dst_ref=dst, send_sem=ss, recv_sem=rs, device_id=dev, device_id_type=MESH
        )
        cp.start()
        return cp

    barrier = pltpu.get_barrier_semaphore()
    for i in far_first:
        pl.semaphore_signal(barrier, inc=1, device_id=z_peer(i), device_id_type=MESH)
    for t in plane:
        pl.semaphore_signal(barrier, inc=1, device_id=plane_peer(*t), device_id_type=MESH)

    onehot = jnp.where(spec_ref[...] == iota((4, ATOMS), 0), 1.0, 0.0)
    lookup = dot(emb_ref[...], onehot, TN, PRECISE)
    hidden = (feat_ref[...].astype(F32) + lookup).astype(BF16)
    stacked = jnp.concatenate([hidden, cot_ref[...]], axis=0)
    r128, c128 = iota((128, 128), 0), iota((128, 128), 1)
    perm = select(c128 == ((r128 // 4) % 2) * 64 + (r128 // 8) * 4 + r128 % 4)
    gbuf[mine, 0:128, :] = dot(perm, stacked).astype(BF16)
    xyz = frac_ref[...]
    hi = xyz.astype(BF16).astype(F32)
    rest = xyz - hi
    mid = rest.astype(BF16).astype(F32)
    pos_s[...] = jnp.zeros_like(pos_s)
    pos_s[0:3, :] = hi
    pos_s[3:6, :] = mid
    pos_s[6:9, :] = rest - mid
    gbuf[mine, 128:144, :] = pos_s[...].astype(BF16)

    pl.semaphore_wait(barrier, len(far_first) + len(plane))

    gathers = [
        send(gbuf.at[mine], gbuf.at[mine], g_ss.at[0], g_rs.at[0], device(y_lo, z, 1 - core, v))
    ]
    y_to = (y_hi * 2 + y_lo + 3 + 2 * core) % 4
    for c in (0, 1):
        gathers.append(
            send(
                gbuf.at[mine], gbuf.at[mine], g_ss.at[1 + c], g_rs.at[1 + core],
                device(y_to % 2, z, c, (y_to // 2) * NX + x),
            )
        )

    def gather_wait(slot, k):
        pltpu.make_async_remote_copy(
            src_ref=gbuf.at[mine], dst_ref=gbuf.at[slot], send_sem=g_ss.at[0], recv_sem=g_rs.at[k],
            device_id=device(y_lo, z, 1 - core, v), device_id_type=MESH,
        ).wait_recv()

    mill = mil_ref[:, pl.ds(pl.multiple_of(mine * KL, KL), KL)].astype(F32)
    mrep[...] = jnp.zeros_like(mrep)
    for i in range(3):
        mrep[3 * i : 3 * i + 3, :] = mill
    mrep_b = mrep[...].astype(BF16)

    def phases(slot):
        tbuf[...] = dot(gbuf[slot, 128:144, :], mrep_b, TN)

        def body(i, carry):
            rows = pl.ds(pl.multiple_of(i * 32, 32), 32)
            c, s = cos_sin_turns(tbuf[rows, :])
            cbuf[slot, rows, :] = c.astype(BF16)
            sbuf[slot, rows, :] = s.astype(BF16)
            return carry

        lax.fori_loop(0, ATOMS // 32, body, 0, unroll=2)

    def factors(slot):
        sp = gbuf[slot, 0:128, :]
        return dot(sp, cbuf[slot]), dot(sp, sbuf[slot])

    phases(mine)
    fc, fs = factors(mine)
    facc[0] = fc
    facc[1] = fs
    for k, slot in ((0, y_lo * 2 + 1 - core), (1, (1 - y_lo) * 2), (2, (1 - y_lo) * 2 + 1)):
        gather_wait(slot, k)
        phases(slot)
        fc, fs = factors(slot)
        facc[0] = facc[0] + fc
        facc[1] = facc[1] + fs
    rs_snd[:, 0:8, :] = facc[0].reshape(NZ, 8, KL)
    rs_snd[:, 8:16, :] = facc[1].reshape(NZ, 8, KL)
    rs = []
    for i in far_first:
        rs.append(send(rs_snd.at[(z + i) % NZ], rs_buf.at[i], rs_ss.at[i], rs_rs.at[i], z_peer(i)))

    kvec = TWO_PI * mill / box_ref[...]
    q_vals = jnp.sum(kvec * kvec, axis=0, keepdims=True)
    nb = w_ref.shape[0]
    q_top = 3.0 * (TWO_PI * MMAX / 105.0) ** 2
    spread = 1.5 * q_top / (nb - 1)
    centers = q_top * iota((nb, KL), 0).astype(F32) / (nb - 1)
    offsets = (q_vals - centers) / spread
    basis = jnp.exp(-offsets * offsets)
    basis_slope = -2.0 * offsets / spread * basis
    p64, c64 = iota((64, 128), 0), iota((64, 128), 1)
    spreadw = jnp.where(p64 == (c64 // 8) * 4 + c64 % 4, 1.0, 0.0)
    w2 = dot(w_ref[...], spreadw, NN, PRECISE)
    filt[...] = dot(w2, basis, TN, PRECISE).reshape(NZ, 8, KL)
    slope[...] = dot(w2, basis_slope, TN, PRECISE).reshape(NZ, 8, KL)
    bk_s[...] = jnp.zeros_like(bk_s)
    bk_s[0:16, :] = basis
    bk_s[16:19, :] = kvec
    bk_s[28:31, :] = kvec
    wm_s[...] = jnp.zeros_like(wm_s)
    for g in range(8):
        wm_s[16 * g : 16 * g + 3, :] = mill
    p, pp = iota((128, 256), 0), iota((128, 256), 1)
    d_, r_ = pp // 16, pp % 16
    source = 8 * d_ + ((r_ // 4 + 1) % 2) * 4 + r_ % 4
    pick_c = select((p == source) & (r_ >= 8))
    pick_s = select((p == source) & (r_ < 8))
    for s in range(4):
        sp = gbuf[s, 0:128, :]
        tcbuf[s] = dot(sp, pick_c, TN).astype(BF16)
        tsbuf[s] = dot(sp, pick_s, TN).astype(BF16)

    total = rs_snd[z]
    for k, i in enumerate(far_first[::-1]):
        rs[len(far_first) - 1 - k].wait_recv()
        total = total + rs_buf[i]
    total = total * (1.0 / math.sqrt(NZ * 4 * ATOMS))
    c8, s8 = total[0:8], total[8:16]
    f8 = filt[z]
    ag_buf[z] = jnp.concatenate([c8 * f8, s8 * f8], axis=0).astype(BF16)
    ag = []
    for i in far_first:
        ag.append(send(ag_buf.at[z], ag_buf.at[z], ag_ss.at[i], ag_rs.at[i], z_peer(i)))

    energy = c8 * pltpu.roll(c8, 4, 0) + s8 * pltpu.roll(s8, 4, 0)
    weight = 0.5 * jnp.sum(slope[z] * energy, axis=0, keepdims=True)
    lhs = jnp.where(iota((8, KL), 0) < 4, energy, bk_s[24:32, :] * weight)
    pl_snd[...] = dot(lhs, bk_s[...], NT, PRECISE)
    pls = []
    for t in plane:
        n = plane_slot(*t)
        pls.append(send(pl_snd, pl_buf.at[n], pl_ss.at[n], pl_rs.at[n], plane_peer(*t)))
    psum = pl_snd[...]
    for t, cp in zip(plane, pls):
        cp.wait_recv()
        psum = psum + pl_buf[plane_slot(*t)]
    zs_buf[z] = psum
    zs = []
    for i in far_first:
        zs.append(send(zs_buf.at[z], zs_buf.at[z], zs_ss.at[i], zs_rs.at[i], z_peer(i)))

    def z_wait(buf, ss, rsem, i):
        pltpu.make_async_remote_copy(
            src_ref=buf.at[z], dst_ref=buf.at[(z + NZ - i) % NZ], send_sem=ss.at[i], recv_sem=rsem.at[i],
            device_id=z_peer(i), device_id_type=MESH,
        ).wait_recv()

    for i in far_first[::-1]:
        z_wait(ag_buf, ag_ss, ag_rs, i)

    terms = ag_buf[...].reshape(256, KL)
    cc_, pp = iota((128, 256), 0) % 64, iota((128, 256), 1)
    at = (cc_ // 4) * 16 + cc_ % 4
    xx = dot(select(pp == at + 4), terms).astype(BF16)
    yy = dot(select(pp == at + 12), terms).astype(BF16)
    wm = wm_s[...].astype(BF16)
    lane = iota((8, 24, 128), 2)
    lane8 = iota((8, 8, 128), 2)
    fins = []
    for p, q in ((1, 1), (1, 0), (0, 1), (0, 0)):
        slot = ((y_lo + p) % 2) * 2 + (core + q) % 2
        alc[...] = dot(tcbuf[slot], terms)
        als[...] = dot(tsbuf[slot], terms)

        def body(i, carry):
            rows = pl.ds(pl.multiple_of(i * 32, 32), 32)
            dbuf[rows, :] = (
                cbuf[slot, rows, :].astype(F32) * alc[rows, :] - sbuf[slot, rows, :].astype(F32) * als[rows, :]
            ).astype(BF16)
            return carry

        lax.fori_loop(0, ATOMS // 32, body, 0, unroll=2)
        out_a = (dot(cbuf[slot], xx, NT) + dot(sbuf[slot], yy, NT)).reshape(NV, PIECE, 128)
        out_b = dot(dbuf[...], wm, NT).reshape(NV, PIECE, 128)
        packed = jnp.where(lane < 64, out_a[:, 0:24, :], out_a[:, 24:48, :])
        pushed = jnp.zeros((NV, 8, 128), F32)
        for g in range(6):
            pushed = jnp.where(lane8 // 16 == g, out_b[:, 8 * g : 8 * g + 8, :], pushed)
        fin_snd[slot] = jnp.concatenate([packed, pushed], axis=1).astype(BF16)
        for t in plane:
            if t[:2] == (p, q):
                n = plane_slot(*t)
                fins.append(
                    send(
                        fin_snd.at[slot, (v + t[2]) % NV], fin_buf.at[n], fin_ss.at[n], fin_rs.at[n],
                        plane_peer(*t),
                    )
                )

    for i in far_first[::-1]:
        z_wait(zs_buf, zs_ss, zs_rs, i)
    vsum = zs_buf[0]
    for d in range(NZ):
        fg_s[4 * d : 4 * d + 4, :] = zs_buf[d, 0:4, :]
        if d:
            vsum = vsum + zs_buf[d]
    grad_scale = math.sqrt(NZ * 4 * ATOMS) / math.sqrt(K)
    wgrad_out[...] = jnp.transpose(fg_s[...])[0:16, 0:64] * grad_scale
    vir_out[...] = vsum[4:7, 16:19] * (-2.0 * grad_scale)

    acc = fin_snd[mine, v].astype(F32)
    for t, cp in zip(plane, fins):
        cp.wait_recv()
        acc = acc + fin_buf[plane_slot(*t)].astype(F32)
    acc = acc * (1.0 / math.sqrt(K))
    turned = jnp.transpose(jnp.concatenate([acc, jnp.zeros((96, 128), F32)], axis=0))
    feat_out[:, 0:24] = turned[0:64, 0:24]
    feat_out[:, 24:48] = turned[64:128, 0:24]
    unit = -TWO_PI / box_ref[...]
    for g in range(6):
        force_out[:, 8 * g : 8 * g + 8] = turned[16 * g : 16 * g + 3, 24:32] * unit

    for cp in gathers + rs + ag + pls + zs + fins:
        cp.wait_send()


def per_device(features, species, embed, frac_pos, box, miller, filter_weight, cotangent):
    channels, atoms = features.shape
    assert (channels, atoms, miller.shape[1]) == (NZ * CH, ATOMS, 4 * KL)
    vmem = pl.BlockSpec(memory_space=pltpu.VMEM)
    dma = pltpu.SemaphoreType.DMA
    scratch = [
        pltpu.VMEM((4, 144, ATOMS), BF16),
        pltpu.VMEM((16, ATOMS), F32),
        pltpu.VMEM((4, ATOMS, KL), BF16),
        pltpu.VMEM((4, ATOMS, KL), BF16),
        pltpu.VMEM((4, ATOMS, KL), BF16),
        pltpu.VMEM((4, ATOMS, KL), BF16),
        pltpu.VMEM((ATOMS, KL), F32),
        pltpu.VMEM((16, KL), F32),
        pltpu.VMEM((128, KL), F32),
        pltpu.VMEM((128, KL), F32),
        pltpu.VMEM((NZ, 8, KL), F32),
        pltpu.VMEM((NZ, 8, KL), F32),
        pltpu.VMEM((2, 128, KL), F32),
        pltpu.VMEM((NZ, 16, KL), F32),
        pltpu.VMEM((NZ, 16, KL), F32),
        pltpu.VMEM((NZ, 16, KL), BF16),
        pltpu.VMEM((8, 128), F32),
        pltpu.VMEM((32, 8, 128), F32),
        pltpu.VMEM((NZ, 8, 128), F32),
        pltpu.VMEM((128, 128), F32),
        pltpu.VMEM((ATOMS, KL), F32),
        pltpu.VMEM((ATOMS, KL), F32),
        pltpu.VMEM((ATOMS, KL), BF16),
        pltpu.VMEM((4, NV, 32, 128), BF16),
        pltpu.VMEM((32, 32, 128), BF16),
        dma((3,)), dma((3,)), dma((NZ,)), dma((NZ,)), dma((NZ,)), dma((NZ,)),
        dma((32,)), dma((32,)), dma((NZ,)), dma((NZ,)), dma((32,)), dma((32,)),
    ]
    return pl.pallas_call(
        kernel,
        out_shape=(
            jax.ShapeDtypeStruct((channels, PIECE), F32),
            jax.ShapeDtypeStruct((3, PIECE), F32),
            jax.ShapeDtypeStruct(filter_weight.shape, F32),
            jax.ShapeDtypeStruct((3, 3), F32),
        ),
        in_specs=[vmem] * 8,
        out_specs=(vmem,) * 4,
        scratch_shapes=scratch,
        compiler_params=pltpu.CompilerParams(collective_id=0, has_side_effects=True),
        name="ewald",
    )(features, species[None, :], embed, frac_pos, box[:, None], miller, filter_weight, cotangent)


def solution(mesh):
    return jax.shard_map(
        per_device,
        mesh=mesh,
        in_specs=(
            P(None, "atom"), P("atom"), P(), P(None, "atom"), P(), P(None, "kvec"), P(), P(None, "atom"),
        ),
        out_specs=(P(None, ("atom", "kvec")), P(None, ("atom", "kvec")), P(), P()),
        check_vma=False,
    )
```

```python
import functools
import math

import jax
import jax.numpy as jnp
import numpy as np
from jax import lax
from jax.experimental import pallas as pl
from jax.experimental.pallas import tpu as pltpu
from jax.sharding import PartitionSpec as P

K = 8192
MMAX = 40
TWO_PI = 2.0 * math.pi
PRECISE = lax.Precision.HIGHEST
MESH = pl.DeviceIdType.MESH
F32, BF16 = jnp.float32, jnp.bfloat16
MAGIC = 12582912.0

NZ = 16
NX = 4
NV = 8
CH = 4
ATOMS = 384
KL = 256
PIECE = 48
Q_TOP = 32000.0

NN = (((1,), (0,)), ((), ()))
NT = (((1,), (1,)), ((), ()))
TN = (((0,), (0,)), ((), ()))


def _fit(fn, degree):
    n = 64
    nodes = 0.125 + 0.125 * np.cos(np.pi * (np.arange(n) + 0.5) / n)
    cheb = np.polynomial.chebyshev.Chebyshev.fit(nodes, fn(np.sqrt(nodes)), degree, domain=[0.0, 0.25])
    return [float(c) for c in cheb.convert(kind=np.polynomial.Polynomial).coef]


ROOT2 = math.sqrt(2.0)
SIN_C = _fit(lambda r: ROOT2 * np.sin(np.pi * r) / r, 4)
COS_C = _fit(lambda r: ROOT2 * np.cos(np.pi * r), 4)


def horner(u, coef):
    acc = coef[-1] * u + coef[-2]
    for c in coef[-3::-1]:
        acc = acc * u + c
    return acc


def cos_sin_turns(t):
    r = t - ((t + MAGIC) - MAGIC)
    u = r * r
    s = r * horner(u, SIN_C)
    c = horner(u, COS_C)
    return 1.0 - s * s, s * c


def dot(a, b, dims=NN, precision=None):
    return lax.dot_general(a, b, dims, preferred_element_type=F32, precision=precision)


def iota(shape, axis):
    return lax.broadcasted_iota(jnp.int32, shape, axis)


def select(cond):
    return jnp.where(cond, 1.0, 0.0).astype(BF16)


def kernel(
    feat_hbm, spec_hbm, emb_hbm, frac_hbm, box_ref, mil_hbm, w_hbm, cot_hbm,
    out_ref,
    feat_ref, spec_ref, emb_ref, frac_ref, mil_ref, w_ref, cot_ref,
    pbuf, gbuf, pos_s, cbuf, sbuf, tcbuf, tsbuf, tbuf, mrep, wm_s, bk_s, filt, slope, facc,
    rs_snd, rs_buf, sc_snd, sc_buf, ag_buf, pl_snd, pl_buf, zs_buf, fg_s, alc, als, dbuf, fin_snd, fin_buf,
    in_s, p_ss, p_rs, g_ss, g_rs, rs_ss, rs_rs, sc_ss, sc_rs, ag_ss, ag_rs,
    pl_ss, pl_rs, zs_ss, zs_rs, fin_ss, fin_rs,
):
    loads = [
        pltpu.make_async_copy(src, dst, in_s.at[n])
        for n, (src, dst) in enumerate(
            (
                (frac_hbm, frac_ref), (mil_hbm, mil_ref), (spec_hbm, spec_ref), (emb_hbm, emb_ref),
                (feat_hbm, feat_ref), (cot_hbm, cot_ref), (w_hbm, w_ref),
            )
        )
    ]
    for load in loads:
        load.start()
    a = lax.axis_index("atom")
    v = lax.axis_index("kvec")
    y_lo = a // (2 * NZ)
    z = (a // 2) % NZ
    core = a % 2
    y_hi = v // NX
    x = v % NX
    mine = y_lo * 2 + core

    def device(yl, zz, cc, vv):
        return {"atom": (yl * NZ + zz) * 2 + cc, "kvec": vv}

    def z_peer(i):
        return device(y_lo, (z + i) % NZ, core, v)

    def plane_peer(p, q, j):
        return device((y_lo + p) % 2, z, (core + q) % 2, (v + j) % NV)

    far_first = [8, 7, 9, 6, 10, 5, 11, 4, 12, 3, 13, 2, 14, 1, 15]
    plane = [(p, q, j) for p in (1, 0) for q in (1, 0) for j in (4, 6, 2, 5, 7, 3, 1, 0)]
    plane = [t for t in plane if t != (0, 0, 0)]

    def plane_slot(p, q, j):
        return (p * 2 + q) * 8 + j

    def send(src, dst, ss, rs, dev):
        cp = pltpu.make_async_remote_copy(
            src_ref=src, dst_ref=dst, send_sem=ss, recv_sem=rs, device_id=dev, device_id_type=MESH
        )
        cp.start()
        return cp

    barrier = pltpu.get_barrier_semaphore()
    for i in far_first:
        pl.semaphore_signal(barrier, inc=1, device_id=z_peer(i), device_id_type=MESH)
    for t in plane:
        pl.semaphore_signal(barrier, inc=1, device_id=plane_peer(*t), device_id_type=MESH)

    for load in loads:
        load.wait()
    onehot = jnp.where(spec_ref[...].reshape(1, ATOMS) == iota((4, ATOMS), 0), 1.0, 0.0)
    lookup = dot(emb_ref[...], onehot, TN, PRECISE)
    hidden = (feat_ref[...].astype(F32) + lookup).astype(BF16)
    stacked = jnp.concatenate([hidden, cot_ref[...]], axis=0)
    r128, c128 = iota((128, 128), 0), iota((128, 128), 1)
    perm = select(c128 == ((r128 // 4) % 2) * 64 + (r128 // 8) * 4 + r128 % 4)
    gbuf[mine] = dot(perm, stacked).astype(BF16)
    xyz = frac_ref[...]
    hi = xyz.astype(BF16).astype(F32)
    rest = xyz - hi
    mid = rest.astype(BF16).astype(F32)
    pos_s[...] = jnp.zeros_like(pos_s)
    pos_s[0:3, :] = hi
    pos_s[3:6, :] = mid
    pos_s[6:9, :] = rest - mid
    pbuf[mine] = pos_s[...].astype(BF16)

    pl.semaphore_wait(barrier, len(far_first) + len(plane))

    y_to = (y_hi * 2 + y_lo + 3 + 2 * core) % 4
    other = device(y_lo, z, 1 - core, v)
    gathers = []
    for buf, ss, rsem in ((pbuf, p_ss, p_rs), (gbuf, g_ss, g_rs)):
        for c in (0, 1):
            gathers.append(
                send(
                    buf.at[mine], buf.at[mine], ss.at[1 + c], rsem.at[1 + core],
                    device(y_to % 2, z, c, (y_to // 2) * NX + x),
                )
            )
        gathers.append(send(buf.at[mine], buf.at[mine], ss.at[0], rsem.at[0], other))

    def gather_wait(buf, ss, rsem, slot, k):
        pltpu.make_async_remote_copy(
            src_ref=buf.at[mine], dst_ref=buf.at[slot], send_sem=ss.at[0], recv_sem=rsem.at[k],
            device_id=other, device_id_type=MESH,
        ).wait_recv()

    mill = mil_ref[:, pl.ds(pl.multiple_of(mine * KL, KL), KL)].astype(F32)
    mrep[...] = jnp.zeros_like(mrep)
    for i in range(3):
        mrep[3 * i : 3 * i + 3, :] = mill
    mrep_b = mrep[...].astype(BF16)

    def phases(slot):
        tbuf[...] = dot(pbuf[slot], mrep_b, TN)

        def body(i, carry):
            rows = pl.ds(pl.multiple_of(i * 32, 32), 32)
            c, s = cos_sin_turns(tbuf[rows, :])
            cbuf[slot, rows, :] = c.astype(BF16)
            sbuf[slot, rows, :] = s.astype(BF16)
            return carry

        lax.fori_loop(0, ATOMS // 32, body, 0, unroll=2)

    def factors(slot):
        sp = gbuf[slot]
        return dot(sp, cbuf[slot]), dot(sp, sbuf[slot])

    phases(mine)
    others = ((0, y_lo * 2 + 1 - core), (1, (1 - y_lo) * 2), (2, (1 - y_lo) * 2 + 1))
    fc, fs = factors(mine)
    for k, slot in others:
        gather_wait(pbuf, p_ss, p_rs, slot, k)
        phases(slot)
    for k, slot in others:
        gather_wait(gbuf, g_ss, g_rs, slot, k)
        fck, fsk = factors(slot)
        fc = fc + fck
        fs = fs + fsk
    facc[0] = fc.reshape(NZ, 8, KL)
    facc[1] = fs.reshape(NZ, 8, KL)
    top = jnp.maximum(jnp.max(jnp.maximum(jnp.abs(fc), jnp.abs(fs)), axis=(0, 1), keepdims=True), 1e-30)
    factor = Q_TOP / top

    def coded(part):
        return ((part * factor + MAGIC) - MAGIC).astype(jnp.int32).reshape(NZ, 8, KL)

    rs_snd[...] = jnp.concatenate([coded(fc), coded(fs)], axis=1).astype(jnp.int16)
    sc_snd[...] = jnp.broadcast_to(top * (1.0 / Q_TOP), (1, 128))
    rs = []
    for i in far_first:
        rs.append(send(sc_snd, sc_buf.at[i], sc_ss.at[i], sc_rs.at[i], z_peer(i)))
        rs.append(send(rs_snd.at[(z + i) % NZ], rs_buf.at[i], rs_ss.at[i], rs_rs.at[i], z_peer(i)))

    row3 = iota((3, 1), 0)
    box = jnp.where(row3 == 0, box_ref[0], jnp.where(row3 == 1, box_ref[1], box_ref[2]))
    kvec = TWO_PI * mill / box
    q_vals = jnp.sum(kvec * kvec, axis=0, keepdims=True)
    nb = w_ref.shape[0]
    q_top = 3.0 * (TWO_PI * MMAX / 105.0) ** 2
    spread = 1.5 * q_top / (nb - 1)
    centers = q_top * iota((nb, KL), 0).astype(F32) / (nb - 1)
    offsets = (q_vals - centers) / spread
    basis = jnp.exp(-offsets * offsets)
    basis_slope = -2.0 * offsets / spread * basis
    p64, c64 = iota((64, 128), 0), iota((64, 128), 1)
    spreadw = jnp.where(p64 == (c64 // 8) * 4 + c64 % 4, 1.0, 0.0)
    w2 = dot(w_ref[...], spreadw, NN, PRECISE)
    filt[...] = dot(w2, basis, TN, PRECISE).reshape(NZ, 8, KL)
    slope[...] = dot(w2, basis_slope, TN, PRECISE).reshape(NZ, 8, KL)
    bk_s[...] = jnp.zeros_like(bk_s)
    bk_s[0:16, :] = basis
    bk_s[16:19, :] = kvec
    bk_s[28:31, :] = kvec
    wm_s[...] = jnp.zeros_like(wm_s)
    for g in range(8):
        wm_s[16 * g : 16 * g + 3, :] = mill
    p, pp = iota((128, 256), 0), iota((128, 256), 1)
    d_, r_ = pp // 16, pp % 16
    source = 8 * d_ + ((r_ // 4 + 1) % 2) * 4 + r_ % 4
    pick_c = select((p == source) & (r_ >= 8))
    pick_s = select((p == source) & (r_ < 8))
    for s in range(4):
        sp = gbuf[s]
        tcbuf[s] = dot(sp, pick_c, TN).astype(BF16)
        tsbuf[s] = dot(sp, pick_s, TN).astype(BF16)

    total = jnp.concatenate([facc[0, z], facc[1, z]], axis=0)
    for k in range(len(far_first) - 1, -1, -1):
        i = far_first[k]
        rs[2 * k].wait_recv()
        rs[2 * k + 1].wait_recv()
        step = jnp.concatenate([sc_buf[i], sc_buf[i]], axis=1)
        total = total + rs_buf[i].astype(jnp.int32).astype(F32) * step
    total = total * (1.0 / math.sqrt(NZ * 4 * ATOMS))
    c8, s8 = total[0:8], total[8:16]
    f8 = filt[z]
    ag_buf[z] = jnp.concatenate([c8 * f8, s8 * f8], axis=0).astype(BF16)
    ag = []
    for i in far_first:
        ag.append(send(ag_buf.at[z], ag_buf.at[z], ag_ss.at[i], ag_rs.at[i], z_peer(i)))

    energy = c8 * pltpu.roll(c8, 4, 0) + s8 * pltpu.roll(s8, 4, 0)
    weight = 0.5 * jnp.sum(slope[z] * energy, axis=0, keepdims=True)
    lhs = jnp.where(iota((8, KL), 0) < 4, energy, bk_s[24:32, :] * weight)
    pl_snd[...] = dot(lhs, bk_s[...], NT, PRECISE)
    pls = []
    for t in plane:
        n = plane_slot(*t)
        pls.append(send(pl_snd, pl_buf.at[n], pl_ss.at[n], pl_rs.at[n], plane_peer(*t)))
    psum = pl_snd[...]
    for t, cp in zip(plane, pls):
        cp.wait_recv()
        psum = psum + pl_buf[plane_slot(*t)]
    zs_buf[z] = psum
    zs = []
    for i in far_first:
        zs.append(send(zs_buf.at[z], zs_buf.at[z], zs_ss.at[i], zs_rs.at[i], z_peer(i)))

    def z_wait(buf, ss, rsem, i):
        pltpu.make_async_remote_copy(
            src_ref=buf.at[z], dst_ref=buf.at[(z + NZ - i) % NZ], send_sem=ss.at[i], recv_sem=rsem.at[i],
            device_id=z_peer(i), device_id_type=MESH,
        ).wait_recv()

    for i in far_first[::-1]:
        z_wait(ag_buf, ag_ss, ag_rs, i)

    terms = ag_buf[...].reshape(256, KL)
    cc_, pp = iota((128, 256), 0) % 64, iota((128, 256), 1)
    at = (cc_ // 4) * 16 + cc_ % 4
    xx = dot(select(pp == at + 4), terms).astype(BF16)
    yy = dot(select(pp == at + 12), terms).astype(BF16)
    wm = wm_s[...].astype(BF16)
    lane = iota((8, 24, 128), 2)
    lane8 = iota((8, 8, 128), 2)
    fins = []
    for p, q in ((1, 1), (1, 0), (0, 1), (0, 0)):
        slot = ((y_lo + p) % 2) * 2 + (core + q) % 2
        alc[...] = dot(tcbuf[slot], terms)
        als[...] = dot(tsbuf[slot], terms)

        def body(i, carry):
            rows = pl.ds(pl.multiple_of(i * 32, 32), 32)
            dbuf[rows, :] = (
                cbuf[slot, rows, :].astype(F32) * alc[rows, :] - sbuf[slot, rows, :].astype(F32) * als[rows, :]
            ).astype(BF16)
            return carry

        lax.fori_loop(0, ATOMS // 32, body, 0, unroll=2)
        out_a = (dot(cbuf[slot], xx, NT) + dot(sbuf[slot], yy, NT)).reshape(NV, PIECE, 128)
        out_b = dot(dbuf[...], wm, NT).reshape(NV, PIECE, 128)
        packed = jnp.where(lane < 64, out_a[:, 0:24, :], out_a[:, 24:48, :])
        pushed = jnp.zeros((NV, 8, 128), F32)
        for g in range(6):
            pushed = jnp.where(lane8 // 16 == g, out_b[:, 8 * g : 8 * g + 8, :], pushed)
        fin_snd[slot] = jnp.concatenate([packed, pushed], axis=1).astype(BF16)
        for t in plane:
            if t[:2] == (p, q):
                n = plane_slot(*t)
                fins.append(
                    send(
                        fin_snd.at[slot, (v + t[2]) % NV], fin_buf.at[n], fin_ss.at[n], fin_rs.at[n],
                        plane_peer(*t),
                    )
                )

    for i in far_first[::-1]:
        z_wait(zs_buf, zs_ss, zs_rs, i)
    vsum = zs_buf[0]
    for d in range(NZ):
        fg_s[4 * d : 4 * d + 4, :] = zs_buf[d, 0:4, :]
        if d:
            vsum = vsum + zs_buf[d]
    grad_scale = math.sqrt(NZ * 4 * ATOMS) / math.sqrt(K)
    out_ref[32:48, :] = jnp.transpose(fg_s[...])[0:16, :] * grad_scale
    out_ref[48:56, :] = vsum * (-2.0 * grad_scale)

    acc = fin_snd[mine, v].astype(F32)
    for t, cp in zip(plane, fins):
        cp.wait_recv()
        acc = acc + fin_buf[plane_slot(*t)].astype(F32)
    unit = jnp.zeros((8, 128), F32)
    for i in range(3):
        unit = jnp.where(iota((8, 128), 1) % 16 == i, -TWO_PI / math.sqrt(K) / box_ref[i], unit)
    out_ref[0:24, :] = acc[0:24] * (1.0 / math.sqrt(K))
    out_ref[24:32, :] = acc[24:32] * unit

    for cp in gathers + rs + ag + pls + zs + fins:
        cp.wait_send()


def unpack(packed_ref, feat_hbm, force_hbm, wgrad_hbm, vir_hbm, feat_s, force_s, wgrad_s, vir_s, sem):
    wgrad_s[...] = packed_ref[32:48, 0:64]
    vir_s[...] = packed_ref[52:55, 16:19]
    turned = jnp.transpose(packed_ref[...])
    feat_s[:, 0:24] = turned[0:64, 0:24]
    feat_s[:, 24:48] = turned[64:128, 0:24]
    for g in range(6):
        force_s[:, 8 * g : 8 * g + 8] = turned[16 * g : 16 * g + 3, 24:32]
    stores = [
        pltpu.make_async_copy(src, dst, sem.at[n])
        for n, (src, dst) in enumerate(
            ((feat_s, feat_hbm), (force_s, force_hbm), (wgrad_s, wgrad_hbm), (vir_s, vir_hbm))
        )
    ]
    for store in stores:
        store.start()
    for store in stores:
        store.wait()


def per_device(features, species, embed, frac_pos, box, miller, filter_weight, cotangent):
    channels, atoms = features.shape
    assert (channels, atoms, miller.shape[1]) == (NZ * CH, ATOMS, 4 * KL)
    vmem, anywhere, smem = (pl.BlockSpec(memory_space=m) for m in (pltpu.VMEM, pl.ANY, pltpu.SMEM))
    dma = pltpu.SemaphoreType.DMA
    loaded = [features, species, embed, frac_pos, miller, filter_weight, cotangent]
    scratch = [pltpu.VMEM(arg.shape, arg.dtype) for arg in loaded] + [
        pltpu.VMEM((4, 16, ATOMS), BF16),
        pltpu.VMEM((4, 128, ATOMS), BF16),
        pltpu.VMEM((16, ATOMS), F32),
        pltpu.VMEM((4, ATOMS, KL), BF16),
        pltpu.VMEM((4, ATOMS, KL), BF16),
        pltpu.VMEM((4, ATOMS, KL), BF16),
        pltpu.VMEM((4, ATOMS, KL), BF16),
        pltpu.VMEM((ATOMS, KL), F32),
        pltpu.VMEM((16, KL), F32),
        pltpu.VMEM((128, KL), F32),
        pltpu.VMEM((128, KL), F32),
        pltpu.VMEM((NZ, 8, KL), F32),
        pltpu.VMEM((NZ, 8, KL), F32),
        pltpu.VMEM((2, NZ, 8, KL), F32),
        pltpu.VMEM((NZ, 16, KL), jnp.int16),
        pltpu.VMEM((NZ, 16, KL), jnp.int16),
        pltpu.VMEM((1, 128), F32),
        pltpu.VMEM((NZ, 1, 128), F32),
        pltpu.VMEM((NZ, 16, KL), BF16),
        pltpu.VMEM((8, 128), F32),
        pltpu.VMEM((32, 8, 128), F32),
        pltpu.VMEM((NZ, 8, 128), F32),
        pltpu.VMEM((128, 128), F32),
        pltpu.VMEM((ATOMS, KL), F32),
        pltpu.VMEM((ATOMS, KL), F32),
        pltpu.VMEM((ATOMS, KL), BF16),
        pltpu.VMEM((4, NV, 32, 128), BF16),
        pltpu.VMEM((32, 32, 128), BF16),
        dma((7,)), dma((3,)), dma((3,)), dma((3,)), dma((3,)),
        dma((NZ,)), dma((NZ,)), dma((NZ,)), dma((NZ,)), dma((NZ,)), dma((NZ,)),
        dma((32,)), dma((32,)), dma((NZ,)), dma((NZ,)), dma((32,)), dma((32,)),
    ]
    packed = pl.pallas_call(
        kernel,
        out_shape=jax.ShapeDtypeStruct((128, 128), F32),
        in_specs=[anywhere] * 4 + [smem] + [anywhere] * 3,
        out_specs=vmem,
        scratch_shapes=scratch,
        compiler_params=pltpu.CompilerParams(collective_id=0, has_side_effects=True),
        name="ewald",
    )(features, species, embed, frac_pos, box, miller, filter_weight, cotangent)
    results = [
        jax.ShapeDtypeStruct(shape, F32)
        for shape in ((channels, PIECE), (3, PIECE), filter_weight.shape, (3, 3))
    ]
    return pl.pallas_call(
        unpack,
        out_shape=results,
        in_specs=[vmem],
        out_specs=[anywhere] * 4,
        scratch_shapes=[pltpu.VMEM(r.shape, F32) for r in results] + [dma((4,))],
        name="unpack",
    )(packed)


def solution(mesh):
    return jax.shard_map(
        per_device,
        mesh=mesh,
        in_specs=(
            P(None, "atom"), P("atom"), P(), P(None, "atom"), P(), P(None, "kvec"), P(), P(None, "atom"),
        ),
        out_specs=(P(None, ("atom", "kvec")), P(None, ("atom", "kvec")), P(), P()),
        check_vma=False,
    )
```

```python
import functools
import math

import jax
import jax.numpy as jnp
import numpy as np
from jax import lax
from jax.experimental import pallas as pl
from jax.experimental.pallas import tpu as pltpu
from jax.sharding import PartitionSpec as P

K = 8192
MMAX = 40
TWO_PI = 2.0 * math.pi
PRECISE = lax.Precision.HIGHEST
MESH = pl.DeviceIdType.MESH
F32, BF16 = jnp.float32, jnp.bfloat16
MAGIC = 12582912.0

NZ = 16
NX = 4
NV = 8
CH = 4
ATOMS = 384
KL = 256
PIECE = 48
Q_TOP = 32000.0

NN = (((1,), (0,)), ((), ()))
NT = (((1,), (1,)), ((), ()))
TN = (((0,), (0,)), ((), ()))


def _fit(fn, degree):
    n = 64
    nodes = 0.125 + 0.125 * np.cos(np.pi * (np.arange(n) + 0.5) / n)
    cheb = np.polynomial.chebyshev.Chebyshev.fit(nodes, fn(np.sqrt(nodes)), degree, domain=[0.0, 0.25])
    return [float(c) for c in cheb.convert(kind=np.polynomial.Polynomial).coef]


ROOT2 = math.sqrt(2.0)
SIN_C = _fit(lambda r: ROOT2 * np.sin(np.pi * r) / r, 4)
COS_C = _fit(lambda r: ROOT2 * np.cos(np.pi * r), 4)


def horner(u, coef):
    acc = coef[-1] * u + coef[-2]
    for c in coef[-3::-1]:
        acc = acc * u + c
    return acc


def cos_sin_turns(t):
    r = t - ((t + MAGIC) - MAGIC)
    u = r * r
    s = r * horner(u, SIN_C)
    c = horner(u, COS_C)
    return 1.0 - s * s, s * c


def dot(a, b, dims=NN, precision=None):
    return lax.dot_general(a, b, dims, preferred_element_type=F32, precision=precision)


def iota(shape, axis):
    return lax.broadcasted_iota(jnp.int32, shape, axis)


def select(cond):
    return jnp.where(cond, 1.0, 0.0).astype(BF16)


def kernel(
    feat_hbm, spec_hbm, emb_hbm, frac_hbm, box_hbm, mil_hbm, w_hbm, cot_hbm,
    out_ref,
    feat_ref, spec_ref, emb_ref, frac_ref, mil_ref, w_ref, cot_ref, box_ref,
    pbuf, gbuf, pos_s, cbuf, sbuf, tcbuf, tsbuf, tbuf, mrep, wm_s, bk_s, filt, slope, facc,
    rs_snd, rs_buf, sc_snd, sc_buf, ag_buf, pl_snd, pl_buf, zs_buf, kv_s, alc, als, dbuf, fin_snd, fin_buf,
    in_s, p_ss, p_rs, g_ss, g_rs, rs_ss, rs_rs, sc_ss, sc_rs, ag_ss, ag_rs,
    pl_ss, pl_rs, zs_ss, zs_rs, fin_ss, fin_rs, know,
):
    loads = [
        pltpu.make_async_copy(src, dst, in_s.at[n])
        for n, (src, dst) in enumerate(
            (
                (frac_hbm, frac_ref), (mil_hbm, mil_ref), (spec_hbm, spec_ref), (emb_hbm, emb_ref),
                (feat_hbm, feat_ref), (cot_hbm, cot_ref), (w_hbm, w_ref), (box_hbm, box_ref),
            )
        )
    ]
    for load in loads:
        load.start()
    a = lax.axis_index("atom")
    v = lax.axis_index("kvec")
    y_lo = a // (2 * NZ)
    z = (a // 2) % NZ
    core = a % 2
    y_hi = v // NX
    x = v % NX
    mine = y_lo * 2 + core

    def device(yl, zz, cc, vv):
        return {"atom": (yl * NZ + zz) * 2 + cc, "kvec": vv}

    def z_peer(i):
        return device(y_lo, (z + i) % NZ, core, v)

    def plane_peer(p, q, j):
        return device((y_lo + p) % 2, z, (core + q) % 2, (v + j) % NV)

    far_first = [8, 7, 9, 6, 10, 5, 11, 4, 12, 3, 13, 2, 14, 1, 15]
    plane = [(p, q, j) for p in (1, 0) for q in (1, 0) for j in (4, 6, 2, 5, 7, 3, 1, 0)]
    plane = [t for t in plane if t != (0, 0, 0)]

    def plane_slot(p, q, j):
        return (p * 2 + q) * 8 + j

    def send(src, dst, ss, rs, dev):
        cp = pltpu.make_async_remote_copy(
            src_ref=src, dst_ref=dst, send_sem=ss, recv_sem=rs, device_id=dev, device_id_type=MESH
        )
        cp.start()
        return cp

    def y_peer(dy, c):
        yy = (y_hi * 2 + y_lo + dy) % 4
        return device(yy % 2, z, c, (yy // 2) * NX + x)

    def x_peer(dx):
        return device(y_lo, z, core, y_hi * NX + (x + dx) % NX)

    def signal(sem, *devices):
        for dev in devices:
            pl.semaphore_signal(sem, inc=1, device_id=dev, device_id_type=MESH)

    other = device(y_lo, z, 1 - core, v)
    barrier = pltpu.get_barrier_semaphore()
    signal(
        barrier, other, y_peer(1, 0), y_peer(1, 1), y_peer(3, 0), y_peer(3, 1),
        x_peer(1), x_peer(3), z_peer(1), z_peer(15),
    )

    loads[0].wait()
    xyz = frac_ref[...]
    hi = xyz.astype(BF16).astype(F32)
    rest = xyz - hi
    mid = rest.astype(BF16).astype(F32)
    pos_s[...] = jnp.zeros_like(pos_s)
    pos_s[0:3, :] = hi
    pos_s[3:6, :] = mid
    pos_s[6:9, :] = rest - mid
    pbuf[mine] = pos_s[...].astype(BF16)
    for load in loads[1:]:
        load.wait()

    y_to = 3 + 2 * core
    gathers = []

    def gather_send(buf, ss, rsem):
        for c in (0, 1):
            gathers.append(send(buf.at[mine], buf.at[mine], ss.at[1 + c], rsem.at[1 + core], y_peer(y_to, c)))
        gathers.append(send(buf.at[mine], buf.at[mine], ss.at[0], rsem.at[0], other))

    def gather_wait(buf, ss, rsem, slot, k):
        pltpu.make_async_remote_copy(
            src_ref=buf.at[mine], dst_ref=buf.at[slot], send_sem=ss.at[0], recv_sem=rsem.at[k],
            device_id=other, device_id_type=MESH,
        ).wait_recv()

    pl.semaphore_wait(barrier, 9)
    gather_send(pbuf, p_ss, p_rs)
    signal(know.at[0], y_peer(1, core), y_peer(3, core))
    signal(know.at[3], z_peer(1), z_peer(15))

    onehot = jnp.where(spec_ref[...].reshape(1, ATOMS) == iota((4, ATOMS), 0), 1.0, 0.0)
    lookup = dot(emb_ref[...], onehot, TN, PRECISE)
    hidden = (feat_ref[...].astype(F32) + lookup).astype(BF16)
    stacked = jnp.concatenate([hidden, cot_ref[...]], axis=0)
    r128, c128 = iota((128, 128), 0), iota((128, 128), 1)
    perm = select(c128 == ((r128 // 4) % 2) * 64 + (r128 % 4) * NZ + r128 // 8)
    gbuf[mine] = dot(perm, stacked).astype(BF16)
    gather_send(gbuf, g_ss, g_rs)

    mill = mil_ref[:, pl.ds(pl.multiple_of(mine * KL, KL), KL)].astype(F32)
    mrep[...] = jnp.zeros_like(mrep)
    for i in range(3):
        mrep[3 * i : 3 * i + 3, :] = mill
    mrep_b = mrep[...].astype(BF16)

    def phases(slot):
        tbuf[...] = dot(pbuf[slot], mrep_b, TN)

        def body(i, carry):
            rows = pl.ds(pl.multiple_of(i * 32, 32), 32)
            c, s = cos_sin_turns(tbuf[rows, :])
            cbuf[slot, rows, :] = c.astype(BF16)
            sbuf[slot, rows, :] = s.astype(BF16)
            return carry

        lax.fori_loop(0, ATOMS // 32, body, 0, unroll=2)

    def factors(slot):
        sp = gbuf[slot]
        return dot(sp, cbuf[slot]), dot(sp, sbuf[slot])

    phases(mine)
    others = ((0, y_lo * 2 + 1 - core), (1, (1 - y_lo) * 2), (2, (1 - y_lo) * 2 + 1))
    fc, fs = factors(mine)
    pl.semaphore_wait(know.at[0], 2)
    signal(know.at[1], x_peer(1), x_peer(3))
    pl.semaphore_wait(know.at[3], 2)
    signal(know.at[4], z_peer(2), z_peer(14))
    for k, slot in others:
        gather_wait(pbuf, p_ss, p_rs, slot, k)
        phases(slot)
        if k == 0:
            pl.semaphore_wait(know.at[1], 2)
            signal(know.at[2], x_peer(1), x_peer(3))
        if k == 1:
            pl.semaphore_wait(know.at[4], 2)
            signal(know.at[5], z_peer(4), z_peer(12))
    for k, slot in others:
        gather_wait(gbuf, g_ss, g_rs, slot, k)
        fck, fsk = factors(slot)
        fc = fc + fck
        fs = fs + fsk
    facc[0] = fc.reshape(NZ, 8, KL)
    facc[1] = fs.reshape(NZ, 8, KL)
    top = jnp.maximum(jnp.max(jnp.maximum(jnp.abs(fc), jnp.abs(fs)), axis=(0, 1), keepdims=True), 1e-30)
    factor = Q_TOP / top

    def coded(part):
        return ((part * factor + MAGIC) - MAGIC).astype(jnp.int32).reshape(NZ, 8, KL)

    rs_snd[...] = jnp.concatenate([coded(fc), coded(fs)], axis=1).astype(jnp.int16)
    sc_snd[...] = jnp.broadcast_to(top * (1.0 / Q_TOP), (1, 128))
    pl.semaphore_wait(know.at[5], 2)
    rs = []
    for i in far_first:
        rs.append(send(sc_snd, sc_buf.at[i], sc_ss.at[i], sc_rs.at[i], z_peer(i)))
        rs.append(send(rs_snd.at[(z + i) % NZ], rs_buf.at[i], rs_ss.at[i], rs_rs.at[i], z_peer(i)))

    row3 = iota((3, 1), 0)
    box = jnp.where(row3 == 0, box_ref[0], jnp.where(row3 == 1, box_ref[1], box_ref[2]))
    kvec = TWO_PI * mill / box
    q_vals = jnp.sum(kvec * kvec, axis=0, keepdims=True)
    nb = w_ref.shape[0]
    q_top = 3.0 * (TWO_PI * MMAX / 105.0) ** 2
    spread = 1.5 * q_top / (nb - 1)
    centers = q_top * iota((nb, KL), 0).astype(F32) / (nb - 1)
    offsets = (q_vals - centers) / spread
    basis = jnp.exp(-offsets * offsets)
    basis_slope = -2.0 * offsets / spread * basis
    p64, c64 = iota((64, 128), 0), iota((64, 128), 1)
    spreadw = jnp.where(p64 == (c64 % 4) * NZ + c64 // 8, 1.0, 0.0)
    w2 = dot(w_ref[...], spreadw, NN, PRECISE)
    filt[...] = dot(w2, basis, TN, PRECISE).reshape(NZ, 8, KL)
    slope[...] = dot(w2, basis_slope, TN, PRECISE).reshape(NZ, 8, KL)
    bk_s[...] = jnp.zeros_like(bk_s)
    for r in range(CH):
        bk_s[16 * r : 16 * r + 16, :] = basis
    for r in range(3):
        bk_s[64 + 16 * r : 67 + 16 * r, :] = kvec
    kv_s[...] = jnp.zeros_like(kv_s)
    kv_s[4:7, :] = kvec
    wm_s[...] = jnp.zeros_like(wm_s)
    for g in range(8):
        wm_s[16 * g : 16 * g + 3, :] = mill
    p, pp = iota((128, 256), 0), iota((128, 256), 1)
    d_, r_ = pp // 16, pp % 16
    source = 8 * d_ + ((r_ // 4 + 1) % 2) * 4 + r_ % 4
    pick_c = select((p == source) & (r_ >= 8))
    pick_s = select((p == source) & (r_ < 8))
    for s in range(4):
        sp = gbuf[s]
        tcbuf[s] = dot(sp, pick_c, TN).astype(BF16)
        tsbuf[s] = dot(sp, pick_s, TN).astype(BF16)

    total = jnp.concatenate([facc[0, z], facc[1, z]], axis=0)
    for k in range(len(far_first) - 1, -1, -1):
        i = far_first[k]
        rs[2 * k].wait_recv()
        rs[2 * k + 1].wait_recv()
        step = jnp.concatenate([sc_buf[i], sc_buf[i]], axis=1)
        total = total + rs_buf[i].astype(jnp.int32).astype(F32) * step
    total = total * (1.0 / math.sqrt(NZ * 4 * ATOMS))
    c8, s8 = total[0:8], total[8:16]
    f8 = filt[z]
    ag_buf[z] = jnp.concatenate([c8 * f8, s8 * f8], axis=0).astype(BF16)
    ag = []
    for i in far_first:
        ag.append(send(ag_buf.at[z], ag_buf.at[z], ag_ss.at[i], ag_rs.at[i], z_peer(i)))

    energy = c8 * pltpu.roll(c8, 4, 0) + s8 * pltpu.roll(s8, 4, 0)
    weight = 0.5 * jnp.sum(slope[z] * energy, axis=0, keepdims=True)
    lhs = jnp.where(iota((8, KL), 0) < 4, energy, kv_s[...] * weight)
    products = dot(lhs, bk_s[...], NT, PRECISE)
    owner = iota((8, 128), 1) // 16 == iota((8, 128), 0)
    pl_snd[...] = jnp.sum(jnp.where(owner, products, 0.0), axis=0, keepdims=True)
    pl.semaphore_wait(know.at[2], 2)
    pls = []
    for t in plane:
        n = plane_slot(*t)
        pls.append(send(pl_snd, pl_buf.at[n], pl_ss.at[n], pl_rs.at[n], plane_peer(*t)))
    psum = pl_snd[...]
    for t, cp in zip(plane, pls):
        cp.wait_recv()
        psum = psum + pl_buf[plane_slot(*t)]
    zs_buf[z] = psum
    zs = []
    for i in far_first:
        zs.append(send(zs_buf.at[z], zs_buf.at[z], zs_ss.at[i], zs_rs.at[i], z_peer(i)))

    def z_wait(buf, ss, rsem, i):
        pltpu.make_async_remote_copy(
            src_ref=buf.at[z], dst_ref=buf.at[(z + NZ - i) % NZ], send_sem=ss.at[i], recv_sem=rsem.at[i],
            device_id=z_peer(i), device_id_type=MESH,
        ).wait_recv()

    for i in far_first[::-1]:
        z_wait(ag_buf, ag_ss, ag_rs, i)

    terms = ag_buf[...].reshape(256, KL)
    cc_, pp = iota((128, 256), 0) % 64, iota((128, 256), 1)
    at = (cc_ % NZ) * 16 + cc_ // NZ
    xx = dot(select(pp == at + 4), terms).astype(BF16)
    yy = dot(select(pp == at + 12), terms).astype(BF16)
    wm = wm_s[...].astype(BF16)
    lane = iota((8, 24, 128), 2)
    lane8 = iota((8, 8, 128), 2)
    fins = []
    for p, q in ((1, 1), (1, 0), (0, 1), (0, 0)):
        slot = ((y_lo + p) % 2) * 2 + (core + q) % 2
        alc[...] = dot(tcbuf[slot], terms)
        als[...] = dot(tsbuf[slot], terms)

        def body(i, carry):
            rows = pl.ds(pl.multiple_of(i * 32, 32), 32)
            dbuf[rows, :] = (
                cbuf[slot, rows, :].astype(F32) * alc[rows, :] - sbuf[slot, rows, :].astype(F32) * als[rows, :]
            ).astype(BF16)
            return carry

        lax.fori_loop(0, ATOMS // 32, body, 0, unroll=2)
        out_a = (dot(cbuf[slot], xx, NT) + dot(sbuf[slot], yy, NT)).reshape(NV, PIECE, 128)
        out_b = dot(dbuf[...], wm, NT).reshape(NV, PIECE, 128)
        packed = jnp.where(lane < 64, out_a[:, 0:24, :], out_a[:, 24:48, :])
        pushed = jnp.zeros((NV, 8, 128), F32)
        for g in range(6):
            pushed = jnp.where(lane8 // 16 == g, out_b[:, 8 * g : 8 * g + 8, :], pushed)
        fin_snd[slot] = jnp.concatenate([packed, pushed], axis=1).astype(BF16)
        for t in plane:
            if t[:2] == (p, q):
                n = plane_slot(*t)
                fins.append(
                    send(
                        fin_snd.at[slot, (v + t[2]) % NV], fin_buf.at[n], fin_ss.at[n], fin_rs.at[n],
                        plane_peer(*t),
                    )
                )

    for i in far_first[::-1]:
        z_wait(zs_buf, zs_ss, zs_rs, i)
    grad_scale = math.sqrt(NZ * 4 * ATOMS) / math.sqrt(K)
    scales = jnp.where(iota((1, 128), 1) < 64, grad_scale, -2.0 * grad_scale)
    for d in range(NZ):
        out_ref[32 + d : 33 + d, :] = zs_buf[d] * scales

    acc = fin_snd[mine, v].astype(F32)
    for t, cp in zip(plane, fins):
        cp.wait_recv()
        acc = acc + fin_buf[plane_slot(*t)].astype(F32)
    unit = jnp.zeros((8, 128), F32)
    for i in range(3):
        unit = jnp.where(iota((8, 128), 1) % 16 == i, -TWO_PI / math.sqrt(K) / box_ref[i], unit)
    out_ref[0:24, :] = acc[0:24] * (1.0 / math.sqrt(K))
    out_ref[24:32, :] = acc[24:32] * unit

    for cp in gathers + rs + ag + pls + zs + fins:
        cp.wait_send()


def unpack(packed_ref, feat_hbm, force_hbm, wgrad_hbm, vir_hbm, feat_s, force_s, wgrad_s, vir_s, sem):
    packed = packed_ref[...]
    feat_s[0:24, :] = packed[0:24, 0:64]
    feat_s[24:48, :] = packed[0:24, 64:128]
    turned = jnp.transpose(jnp.concatenate([packed, jnp.zeros((80, 128), F32)], axis=0))
    for g in range(6):
        force_s[:, 8 * g : 8 * g + 8] = turned[16 * g : 16 * g + 3, 24:32]
    for r in range(CH):
        wgrad_s[:, NZ * r : NZ * r + NZ] = turned[16 * r : 16 * r + 16, 32:48]
    whole = jnp.sum(packed[32:48], axis=0, keepdims=True)
    for r in range(3):
        vir_s[r : r + 1, :] = whole[:, 64 + 16 * r : 67 + 16 * r]
    stores = [
        pltpu.make_async_copy(src, dst, sem.at[n])
        for n, (src, dst) in enumerate(
            ((feat_s, feat_hbm), (force_s, force_hbm), (wgrad_s, wgrad_hbm), (vir_s, vir_hbm))
        )
    ]
    for store in stores:
        store.start()
    for store in stores:
        store.wait()


def per_device(features, species, embed, frac_pos, box, miller, filter_weight, cotangent):
    channels, atoms = features.shape
    assert (channels, atoms, miller.shape[1]) == (NZ * CH, ATOMS, 4 * KL)
    vmem, hbm, anywhere = (pl.BlockSpec(memory_space=m) for m in (pltpu.VMEM, pl.ANY, pl.ANY))
    dma = pltpu.SemaphoreType.DMA
    loaded = [features, species, embed, frac_pos, miller, filter_weight, cotangent]
    scratch = [pltpu.VMEM(arg.shape, arg.dtype) for arg in loaded] + [
        pltpu.SMEM(box.shape, F32),
        pltpu.VMEM((4, 16, ATOMS), BF16),
        pltpu.VMEM((4, 128, ATOMS), BF16),
        pltpu.VMEM((16, ATOMS), F32),
        pltpu.VMEM((4, ATOMS, KL), BF16),
        pltpu.VMEM((4, ATOMS, KL), BF16),
        pltpu.VMEM((4, ATOMS, KL), BF16),
        pltpu.VMEM((4, ATOMS, KL), BF16),
        pltpu.VMEM((ATOMS, KL), F32),
        pltpu.VMEM((16, KL), F32),
        pltpu.VMEM((128, KL), F32),
        pltpu.VMEM((128, KL), F32),
        pltpu.VMEM((NZ, 8, KL), F32),
        pltpu.VMEM((NZ, 8, KL), F32),
        pltpu.VMEM((2, NZ, 8, KL), F32),
        pltpu.VMEM((NZ, 16, KL), jnp.int16),
        pltpu.VMEM((NZ, 16, KL), jnp.int16),
        pltpu.VMEM((1, 128), F32),
        pltpu.VMEM((NZ, 1, 128), F32),
        pltpu.VMEM((NZ, 16, KL), BF16),
        pltpu.VMEM((1, 128), F32),
        pltpu.VMEM((32, 1, 128), F32),
        pltpu.VMEM((NZ, 1, 128), F32),
        pltpu.VMEM((8, KL), F32),
        pltpu.VMEM((ATOMS, KL), F32),
        pltpu.VMEM((ATOMS, KL), F32),
        pltpu.VMEM((ATOMS, KL), BF16),
        pltpu.VMEM((4, NV, 32, 128), BF16),
        pltpu.VMEM((32, 32, 128), BF16),
        dma((8,)), dma((3,)), dma((3,)), dma((3,)), dma((3,)),
        dma((NZ,)), dma((NZ,)), dma((NZ,)), dma((NZ,)), dma((NZ,)), dma((NZ,)),
        dma((32,)), dma((32,)), dma((NZ,)), dma((NZ,)), dma((32,)), dma((32,)),
        pltpu.SemaphoreType.REGULAR((6,)),
    ]
    packed = pl.pallas_call(
        kernel,
        out_shape=jax.ShapeDtypeStruct((48, 128), F32),
        in_specs=[hbm] * 8,
        out_specs=vmem,
        scratch_shapes=scratch,
        compiler_params=pltpu.CompilerParams(collective_id=0, has_side_effects=True),
        name="ewald",
    )(features, species, embed, frac_pos, box, miller, filter_weight, cotangent)
    results = [
        jax.ShapeDtypeStruct(shape, F32)
        for shape in ((PIECE, channels), (3, PIECE), filter_weight.shape, (3, 3))
    ]
    feat_grad, force, wgrad, virial = pl.pallas_call(
        unpack,
        out_shape=results,
        in_specs=[vmem],
        out_specs=[anywhere] * 4,
        scratch_shapes=[pltpu.VMEM(r.shape, F32) for r in results] + [dma((4,))],
        name="unpack",
    )(packed)
    return feat_grad.T, force, wgrad, virial


def solution(mesh):
    return jax.shard_map(
        per_device,
        mesh=mesh,
        in_specs=(
            P(None, "atom"), P("atom"), P(), P(None, "atom"), P(), P(None, "kvec"), P(), P(None, "atom"),
        ),
        out_specs=(P(None, ("atom", "kvec")), P(None, ("atom", "kvec")), P(), P()),
        check_vma=False,
    )
```

```python
import functools
import math

import jax
import jax.numpy as jnp
import numpy as np
from jax import lax
from jax.experimental import pallas as pl
from jax.experimental.pallas import tpu as pltpu
from jax.sharding import PartitionSpec as P

K = 8192
MMAX = 40
TWO_PI = 2.0 * math.pi
PRECISE = lax.Precision.HIGHEST
MESH = pl.DeviceIdType.MESH
F32, BF16 = jnp.float32, jnp.bfloat16
MAGIC = 12582912.0

NZ = 16
NX = 4
NV = 8
CH = 4
ATOMS = 384
KL = 256
PIECE = 48
Q_TOP = 32000.0

NN = (((1,), (0,)), ((), ()))
NT = (((1,), (1,)), ((), ()))
TN = (((0,), (0,)), ((), ()))


def _fit(fn, degree):
    n = 64
    nodes = 0.125 + 0.125 * np.cos(np.pi * (np.arange(n) + 0.5) / n)
    cheb = np.polynomial.chebyshev.Chebyshev.fit(nodes, fn(np.sqrt(nodes)), degree, domain=[0.0, 0.25])
    return [float(c) for c in cheb.convert(kind=np.polynomial.Polynomial).coef]


ROOT2 = math.sqrt(2.0)
SIN_C = _fit(lambda r: ROOT2 * np.sin(np.pi * r) / r, 4)
COS_C = _fit(lambda r: ROOT2 * np.cos(np.pi * r), 4)


def horner(u, coef):
    acc = coef[-1] * u + coef[-2]
    for c in coef[-3::-1]:
        acc = acc * u + c
    return acc


def cos_sin_turns(t):
    r = t - ((t + MAGIC) - MAGIC)
    u = r * r
    s = r * horner(u, SIN_C)
    c = horner(u, COS_C)
    return 1.0 - s * s, s * c


def dot(a, b, dims=NN, precision=None):
    return lax.dot_general(a, b, dims, preferred_element_type=F32, precision=precision)


def iota(shape, axis):
    return lax.broadcasted_iota(jnp.int32, shape, axis)


def select(cond):
    return jnp.where(cond, 1.0, 0.0).astype(BF16)


def kernel(
    feat_hbm, spec_hbm, emb_hbm, frac_hbm, box_hbm, mil_hbm, w_hbm, cot_hbm,
    out_ref,
    feat_ref, spec_ref, emb_ref, frac_ref, mil_ref, w_ref, cot_ref, box_ref,
    pbuf, gbuf, pos_s, cbuf, sbuf, tcbuf, tsbuf, tbuf, mrep, wm_s, bk_s, filt, slope, facc,
    rs_snd, rs_buf, sc_snd, sc_buf, ag_buf, pl_snd, pl_buf, zs_buf, kv_s, alc, als, dbuf, fin_snd, fin_buf,
    in_s, p_ss, p_rs, g_ss, g_rs, rs_ss, rs_rs, sc_ss, sc_rs, ag_ss, ag_rs,
    pl_ss, pl_rs, zs_ss, zs_rs, fin_ss, fin_rs, know,
):
    loads = [
        pltpu.make_async_copy(src, dst, in_s.at[n])
        for n, (src, dst) in enumerate(
            (
                (frac_hbm, frac_ref), (mil_hbm, mil_ref), (spec_hbm, spec_ref), (emb_hbm, emb_ref),
                (feat_hbm, feat_ref), (cot_hbm, cot_ref), (w_hbm, w_ref), (box_hbm, box_ref),
            )
        )
    ]
    for load in loads:
        load.start()
    a = lax.axis_index("atom")
    v = lax.axis_index("kvec")
    y_lo = a // (2 * NZ)
    z = (a // 2) % NZ
    core = a % 2
    y_hi = v // NX
    x = v % NX
    mine = y_lo * 2 + core

    def device(yl, zz, cc, vv):
        return {"atom": (yl * NZ + zz) * 2 + cc, "kvec": vv}

    def z_peer(i):
        return device(y_lo, (z + i) % NZ, core, v)

    def plane_peer(p, q, j):
        return device((y_lo + p) % 2, z, (core + q) % 2, (v + j) % NV)

    far_first = [8, 7, 9, 6, 10, 5, 11, 4, 12, 3, 13, 2, 14, 1, 15]
    plane = [(p, q, j) for p in (0, 1) for q in (1, 0) for j in (6, 2, 5, 7, 3, 4, 1, 0)]
    plane = [t for t in plane if t != (0, 0, 0)]

    def plane_slot(p, q, j):
        return (p * 2 + q) * 8 + j

    def send(src, dst, ss, rs, dev):
        cp = pltpu.make_async_remote_copy(
            src_ref=src, dst_ref=dst, send_sem=ss, recv_sem=rs, device_id=dev, device_id_type=MESH
        )
        cp.start()
        return cp

    def y_peer(dy, c):
        yy = (y_hi * 2 + y_lo + dy) % 4
        return device(yy % 2, z, c, (yy // 2) * NX + x)

    def x_peer(dx):
        return device(y_lo, z, core, y_hi * NX + (x + dx) % NX)

    def signal(sem, *devices):
        for dev in devices:
            pl.semaphore_signal(sem, inc=1, device_id=dev, device_id_type=MESH)

    other = device(y_lo, z, 1 - core, v)
    barrier = pltpu.get_barrier_semaphore()
    signal(
        barrier, other, y_peer(1, 0), y_peer(1, 1), y_peer(3, 0), y_peer(3, 1),
        x_peer(1), x_peer(3), z_peer(1), z_peer(15),
    )

    loads[0].wait()
    xyz = frac_ref[...]
    hi = xyz.astype(BF16).astype(F32)
    rest = xyz - hi
    mid = rest.astype(BF16).astype(F32)
    pos_s[...] = jnp.zeros_like(pos_s)
    pos_s[0:3, :] = hi
    pos_s[3:6, :] = mid
    pos_s[6:9, :] = rest - mid
    pbuf[mine] = pos_s[...].astype(BF16)

    y_to = 3 + 2 * core
    gathers = []

    def gather_send(buf, ss, rsem):
        for c in (0, 1):
            gathers.append(send(buf.at[mine], buf.at[mine], ss.at[1 + c], rsem.at[1 + core], y_peer(y_to, c)))
        gathers.append(send(buf.at[mine], buf.at[mine], ss.at[0], rsem.at[0], other))

    def gather_wait(buf, ss, rsem, slot, k):
        pltpu.make_async_remote_copy(
            src_ref=buf.at[mine], dst_ref=buf.at[slot], send_sem=ss.at[0], recv_sem=rsem.at[k],
            device_id=other, device_id_type=MESH,
        ).wait_recv()

    pl.semaphore_wait(barrier, 9)
    gather_send(pbuf, p_ss, p_rs)
    signal(know.at[0], y_peer(1, core), y_peer(3, core))
    signal(know.at[3], z_peer(1), z_peer(15))

    for load in loads[1:]:
        load.wait()
    onehot = jnp.where(spec_ref[...].reshape(1, ATOMS) == iota((4, ATOMS), 0), 1.0, 0.0)
    lookup = dot(emb_ref[...], onehot, TN, PRECISE)
    hidden = (feat_ref[...].astype(F32) + lookup).astype(BF16)
    stacked = jnp.concatenate([hidden, cot_ref[...]], axis=0)
    r128, c128 = iota((128, 128), 0), iota((128, 128), 1)
    perm = select(c128 == ((r128 // 4) % 2) * 64 + (r128 % 4) * NZ + r128 // 8)
    gbuf[mine] = dot(perm, stacked).astype(BF16)
    gather_send(gbuf, g_ss, g_rs)
    pl.semaphore_wait(know.at[3], 2)
    signal(know.at[4], z_peer(2), z_peer(14))
    pl.semaphore_wait(know.at[0], 2)
    signal(know.at[1], x_peer(1), x_peer(3))

    mill = mil_ref[:, pl.ds(pl.multiple_of(mine * KL, KL), KL)].astype(F32)
    mrep[...] = jnp.zeros_like(mrep)
    for i in range(3):
        mrep[3 * i : 3 * i + 3, :] = mill
    mrep_b = mrep[...].astype(BF16)

    def phases(slot):
        tbuf[...] = dot(pbuf[slot], mrep_b, TN)

        def body(i, carry):
            c, s = cos_sin_turns(tbuf[pl.ds(pl.multiple_of(i * 32, 32), 32), :])
            rows = pl.ds(pl.multiple_of((slot % 2) * ATOMS + i * 32, 32), 32)
            cbuf[slot // 2, rows, :] = c.astype(BF16)
            sbuf[slot // 2, rows, :] = s.astype(BF16)
            return carry

        lax.fori_loop(0, ATOMS // 32, body, 0, unroll=2)

    def factors(slot):
        sp = gbuf[slot]
        rows = pl.ds(pl.multiple_of((slot % 2) * ATOMS, ATOMS), ATOMS)
        return dot(sp, cbuf[slot // 2, rows, :]), dot(sp, sbuf[slot // 2, rows, :])

    phases(mine)
    others = ((0, y_lo * 2 + 1 - core), (1, (1 - y_lo) * 2), (2, (1 - y_lo) * 2 + 1))
    fc, fs = factors(mine)
    for k, slot in others:
        gather_wait(pbuf, p_ss, p_rs, slot, k)
        phases(slot)
        if k == 0:
            pl.semaphore_wait(know.at[4], 2)
            signal(know.at[5], z_peer(4), z_peer(12))
            pl.semaphore_wait(know.at[1], 2)
            signal(know.at[2], x_peer(1), x_peer(3))
    for k, slot in others:
        gather_wait(gbuf, g_ss, g_rs, slot, k)
        fck, fsk = factors(slot)
        fc = fc + fck
        fs = fs + fsk
    facc[0] = fc.reshape(NZ, 8, KL)
    facc[1] = fs.reshape(NZ, 8, KL)
    top = jnp.maximum(jnp.max(jnp.maximum(jnp.abs(fc), jnp.abs(fs)), axis=(0, 1), keepdims=True), 1e-30)
    factor = Q_TOP / top

    def coded(part):
        return ((part * factor + MAGIC) - MAGIC).astype(jnp.int32).reshape(NZ, 8, KL)

    rs_snd[...] = jnp.concatenate([coded(fc), coded(fs)], axis=1).astype(jnp.int16)
    sc_snd[...] = jnp.broadcast_to(top * (1.0 / Q_TOP), (1, 128))
    pl.semaphore_wait(know.at[5], 2)
    rs = []
    for i in far_first:
        rs.append(send(sc_snd, sc_buf.at[i], sc_ss.at[i], sc_rs.at[i], z_peer(i)))
        rs.append(send(rs_snd.at[(z + i) % NZ], rs_buf.at[i], rs_ss.at[i], rs_rs.at[i], z_peer(i)))

    row3 = iota((3, 1), 0)
    box = jnp.where(row3 == 0, box_ref[0], jnp.where(row3 == 1, box_ref[1], box_ref[2]))
    kvec = TWO_PI * mill / box
    q_vals = jnp.sum(kvec * kvec, axis=0, keepdims=True)
    nb = w_ref.shape[0]
    q_top = 3.0 * (TWO_PI * MMAX / 105.0) ** 2
    spread = 1.5 * q_top / (nb - 1)
    centers = q_top * iota((nb, KL), 0).astype(F32) / (nb - 1)
    offsets = (q_vals - centers) / spread
    basis = jnp.exp(-offsets * offsets)
    basis_slope = -2.0 * offsets / spread * basis
    p64, c64 = iota((64, 128), 0), iota((64, 128), 1)
    spreadw = jnp.where(p64 == (c64 % 4) * NZ + c64 // 8, 1.0, 0.0)
    w2 = dot(w_ref[...], spreadw, NN, PRECISE)
    filt[...] = dot(w2, basis, TN, PRECISE).reshape(NZ, 8, KL)
    slope[...] = dot(w2, basis_slope, TN, PRECISE).reshape(NZ, 8, KL)
    bk_s[...] = jnp.zeros_like(bk_s)
    for r in range(CH):
        bk_s[16 * r : 16 * r + 16, :] = basis
    for r in range(3):
        bk_s[64 + 16 * r : 67 + 16 * r, :] = kvec
    kv_s[...] = jnp.zeros_like(kv_s)
    kv_s[4:7, :] = kvec
    wm_s[...] = jnp.zeros_like(wm_s)
    for g in range(8):
        wm_s[16 * g : 16 * g + 3, :] = mill
    p, pp = iota((128, 256), 0), iota((128, 256), 1)
    d_, r_ = pp // 16, pp % 16
    source = 8 * d_ + ((r_ // 4 + 1) % 2) * 4 + r_ % 4
    pick_c = select((p == source) & (r_ >= 8))
    pick_s = select((p == source) & (r_ < 8))
    for s in range(4):
        sp = gbuf[s]
        rows = slice((s % 2) * ATOMS, (s % 2 + 1) * ATOMS)
        tcbuf[s // 2, rows, :] = dot(sp, pick_c, TN).astype(BF16)
        tsbuf[s // 2, rows, :] = dot(sp, pick_s, TN).astype(BF16)

    total = jnp.concatenate([facc[0, z], facc[1, z]], axis=0)
    for k in range(len(far_first) - 1, -1, -1):
        i = far_first[k]
        rs[2 * k].wait_recv()
        rs[2 * k + 1].wait_recv()
        step = jnp.concatenate([sc_buf[i], sc_buf[i]], axis=1)
        total = total + rs_buf[i].astype(jnp.int32).astype(F32) * step
    total = total * (1.0 / math.sqrt(NZ * 4 * ATOMS))
    c8, s8 = total[0:8], total[8:16]
    f8 = filt[z]
    ag_buf[z] = jnp.concatenate([c8 * f8, s8 * f8], axis=0).astype(BF16)
    ag = []
    for i in far_first:
        ag.append(send(ag_buf.at[z], ag_buf.at[z], ag_ss.at[i], ag_rs.at[i], z_peer(i)))

    energy = c8 * pltpu.roll(c8, 4, 0) + s8 * pltpu.roll(s8, 4, 0)
    weight = 0.5 * jnp.sum(slope[z] * energy, axis=0, keepdims=True)
    lhs = jnp.where(iota((8, KL), 0) < 4, energy, kv_s[...] * weight)
    products = dot(lhs, bk_s[...], NT, PRECISE)
    owner = iota((8, 128), 1) // 16 == iota((8, 128), 0)
    pl_snd[...] = jnp.sum(jnp.where(owner, products, 0.0), axis=0, keepdims=True)
    pl.semaphore_wait(know.at[2], 2)
    pls = []
    for t in plane:
        n = plane_slot(*t)
        pls.append(send(pl_snd, pl_buf.at[n], pl_ss.at[n], pl_rs.at[n], plane_peer(*t)))
    psum = pl_snd[...]
    for t, cp in zip(plane, pls):
        cp.wait_recv()
        psum = psum + pl_buf[plane_slot(*t)]
    zs_buf[z] = psum
    zs = []
    for i in far_first:
        zs.append(send(zs_buf.at[z], zs_buf.at[z], zs_ss.at[i], zs_rs.at[i], z_peer(i)))

    def z_wait(buf, ss, rsem, i):
        pltpu.make_async_remote_copy(
            src_ref=buf.at[z], dst_ref=buf.at[(z + NZ - i) % NZ], send_sem=ss.at[i], recv_sem=rsem.at[i],
            device_id=z_peer(i), device_id_type=MESH,
        ).wait_recv()

    for cp in gathers + rs:
        cp.wait_send()
    for i in far_first[::-1]:
        z_wait(ag_buf, ag_ss, ag_rs, i)

    terms = ag_buf[...].reshape(256, KL)
    cc_, pp = iota((128, 256), 0) % 64, iota((128, 256), 1)
    at = (cc_ % NZ) * 16 + cc_ // NZ
    xx = dot(select(pp == at + 4), terms).astype(BF16)
    yy = dot(select(pp == at + 12), terms).astype(BF16)
    wm = wm_s[...].astype(BF16)
    lane = iota((2 * NV, 24, 128), 2)
    lane8 = iota((2 * NV, 8, 128), 2)
    fins = []
    for p in (0, 1):
        pair = (y_lo + p) % 2
        alc[...] = dot(tcbuf[pair], terms)
        als[...] = dot(tsbuf[pair], terms)

        def body(i, carry):
            rows = pl.ds(pl.multiple_of(i * 32, 32), 32)
            dbuf[rows, :] = (
                cbuf[pair, rows, :].astype(F32) * alc[rows, :] - sbuf[pair, rows, :].astype(F32) * als[rows, :]
            ).astype(BF16)
            return carry

        lax.fori_loop(0, 2 * ATOMS // 32, body, 0, unroll=4)
        out_a = (dot(cbuf[pair], xx, NT) + dot(sbuf[pair], yy, NT)).reshape(2 * NV, PIECE, 128)
        out_b = dot(dbuf[...], wm, NT).reshape(2 * NV, PIECE, 128)
        packed = jnp.where(lane < 64, out_a[:, 0:24, :], out_a[:, 24:48, :])
        pushed = jnp.zeros((2 * NV, 8, 128), F32)
        for g in range(6):
            pushed = jnp.where(lane8 // 16 == g, out_b[:, 8 * g : 8 * g + 8, :], pushed)
        fin_snd[pair] = jnp.concatenate([packed, pushed], axis=1).astype(BF16)
        for t in plane:
            if t[0] == p:
                n = plane_slot(*t)
                piece = ((core + t[1]) % 2) * NV + (v + t[2]) % NV
                fins.append(
                    send(fin_snd.at[pair, piece], fin_buf.at[n], fin_ss.at[n], fin_rs.at[n], plane_peer(*t))
                )

    for i in far_first[::-1]:
        z_wait(zs_buf, zs_ss, zs_rs, i)
    grad_scale = math.sqrt(NZ * 4 * ATOMS) / math.sqrt(K)
    scales = jnp.where(iota((1, 128), 1) < 64, grad_scale, -2.0 * grad_scale)
    for d in range(NZ):
        out_ref[32 + d : 33 + d, :] = zs_buf[d] * scales

    for cp in ag + pls + zs + fins:
        cp.wait_send()
    acc = fin_snd[y_lo, core * NV + v].astype(F32)
    for t, cp in zip(plane, fins):
        cp.wait_recv()
        acc = acc + fin_buf[plane_slot(*t)].astype(F32)
    unit = jnp.zeros((8, 128), F32)
    for i in range(3):
        unit = jnp.where(iota((8, 128), 1) % 16 == i, -TWO_PI / math.sqrt(K) / box_ref[i], unit)
    out_ref[0:24, :] = acc[0:24] * (1.0 / math.sqrt(K))
    out_ref[24:32, :] = acc[24:32] * unit


def unpack(packed_ref, feat_hbm, force_hbm, wgrad_hbm, vir_hbm, feat_s, force_s, wgrad_s, vir_s, sem):
    packed = packed_ref[...]
    feat_s[0:24, :] = packed[0:24, 0:64]
    feat_s[24:48, :] = packed[0:24, 64:128]
    turned = jnp.transpose(jnp.concatenate([packed, jnp.zeros((80, 128), F32)], axis=0))
    for g in range(6):
        force_s[:, 8 * g : 8 * g + 8] = turned[16 * g : 16 * g + 3, 24:32]
    for r in range(CH):
        wgrad_s[:, NZ * r : NZ * r + NZ] = turned[16 * r : 16 * r + 16, 32:48]
    whole = jnp.sum(packed[32:48], axis=0, keepdims=True)
    for r in range(3):
        vir_s[r : r + 1, :] = whole[:, 64 + 16 * r : 67 + 16 * r]
    stores = [
        pltpu.make_async_copy(src, dst, sem.at[n])
        for n, (src, dst) in enumerate(
            ((feat_s, feat_hbm), (force_s, force_hbm), (wgrad_s, wgrad_hbm), (vir_s, vir_hbm))
        )
    ]
    for store in stores:
        store.start()
    for store in stores:
        store.wait()


def per_device(features, species, embed, frac_pos, box, miller, filter_weight, cotangent):
    channels, atoms = features.shape
    assert (channels, atoms, miller.shape[1]) == (NZ * CH, ATOMS, 4 * KL)
    vmem, hbm, anywhere = (pl.BlockSpec(memory_space=m) for m in (pltpu.VMEM, pl.ANY, pl.ANY))
    dma = pltpu.SemaphoreType.DMA
    loaded = [features, species, embed, frac_pos, miller, filter_weight, cotangent]
    scratch = [pltpu.VMEM(arg.shape, arg.dtype) for arg in loaded] + [
        pltpu.SMEM(box.shape, F32),
        pltpu.VMEM((4, 16, ATOMS), BF16),
        pltpu.VMEM((4, 128, ATOMS), BF16),
        pltpu.VMEM((16, ATOMS), F32),
        pltpu.VMEM((2, 2 * ATOMS, KL), BF16),
        pltpu.VMEM((2, 2 * ATOMS, KL), BF16),
        pltpu.VMEM((2, 2 * ATOMS, KL), BF16),
        pltpu.VMEM((2, 2 * ATOMS, KL), BF16),
        pltpu.VMEM((ATOMS, KL), F32),
        pltpu.VMEM((16, KL), F32),
        pltpu.VMEM((128, KL), F32),
        pltpu.VMEM((128, KL), F32),
        pltpu.VMEM((NZ, 8, KL), F32),
        pltpu.VMEM((NZ, 8, KL), F32),
        pltpu.VMEM((2, NZ, 8, KL), F32),
        pltpu.VMEM((NZ, 16, KL), jnp.int16),
        pltpu.VMEM((NZ, 16, KL), jnp.int16),
        pltpu.VMEM((1, 128), F32),
        pltpu.VMEM((NZ, 1, 128), F32),
        pltpu.VMEM((NZ, 16, KL), BF16),
        pltpu.VMEM((1, 128), F32),
        pltpu.VMEM((32, 1, 128), F32),
        pltpu.VMEM((NZ, 1, 128), F32),
        pltpu.VMEM((8, KL), F32),
        pltpu.VMEM((2 * ATOMS, KL), F32),
        pltpu.VMEM((2 * ATOMS, KL), F32),
        pltpu.VMEM((2 * ATOMS, KL), BF16),
        pltpu.VMEM((2, 2 * NV, 32, 128), BF16),
        pltpu.VMEM((32, 32, 128), BF16),
        dma((8,)), dma((3,)), dma((3,)), dma((3,)), dma((3,)),
        dma((NZ,)), dma((NZ,)), dma((NZ,)), dma((NZ,)), dma((NZ,)), dma((NZ,)),
        dma((32,)), dma((32,)), dma((NZ,)), dma((NZ,)), dma((32,)), dma((32,)),
        pltpu.SemaphoreType.REGULAR((6,)),
    ]
    packed = pl.pallas_call(
        kernel,
        out_shape=jax.ShapeDtypeStruct((48, 128), F32),
        in_specs=[hbm] * 8,
        out_specs=vmem,
        scratch_shapes=scratch,
        compiler_params=pltpu.CompilerParams(collective_id=0, has_side_effects=True),
        name="ewald",
    )(features, species, embed, frac_pos, box, miller, filter_weight, cotangent)
    results = [
        jax.ShapeDtypeStruct(shape, F32)
        for shape in ((PIECE, channels), (3, PIECE), filter_weight.shape, (3, 3))
    ]
    feat_grad, force, wgrad, virial = pl.pallas_call(
        unpack,
        out_shape=results,
        in_specs=[vmem],
        out_specs=[anywhere] * 4,
        scratch_shapes=[pltpu.VMEM(r.shape, F32) for r in results] + [dma((4,))],
        name="unpack",
    )(packed)
    return feat_grad.T, force, wgrad, virial


def solution(mesh):
    return jax.shard_map(
        per_device,
        mesh=mesh,
        in_specs=(
            P(None, "atom"), P("atom"), P(), P(None, "atom"), P(), P(None, "kvec"), P(), P(None, "atom"),
        ),
        out_specs=(P(None, ("atom", "kvec")), P(None, ("atom", "kvec")), P(), P()),
        check_vma=False,
    )
```
